512 devices in a mesh: slide: 8 (over y, core), seq: 16 (over z), rep: 4 (over x).
Axes of the slice: x: 4, y: 4, z: 16, core: 2. Of those that a mesh axis runs over, the one named last changes fastest.
Arguments:
- tile_feats: bfloat16 [128, 128, 8, 1536], P(('slide', 'seq'), None, None, 'rep'), may hold values from -6 to 6
- tile_counts: int32 [8, 16, 128], P('slide'), may hold values from 0 to 8, as said below
- in_weight: bfloat16 [1536, 768], P('rep'), may hold values from -0.16871811 to 0.16871811
- norm_gain: float32 [768], replicated, may hold values from 0.1 to 1.9
- qkv_weight: bfloat16 [768, 3, 768], P(None, None, 'rep'), may hold values from -0.39687289 to 0.39687289
- out_weight: bfloat16 [768, 768], P('rep'), may hold values from -0.21875 to 0.21875
- final_gain: float32 [768], replicated, may hold values from 0.1 to 1.9
- reports: bfloat16 [1024, 768], P('rep'), may hold values from -6 to 6
- report_pair: int32 [8], P('slide'), may hold values from 0 to 1023
Outputs:
- head_out: float32 [8, 8192, 768], P('slide', 'seq', 'rep')
- slide_emb: float32 [8, 768], P('slide')
- losses: float32 [8], P('slide')
The draws below stay inside these ranges and needn't reach their ends.
Inputs may be any that keep to these rules, and one draw needn't show every extreme that they name: tile_counts[s, j, src] is what source src sends to block j of slide s. Sources 2k and 2k + 1 together send at most 8 to one block, so that one block receives at most 512 tiles and at least 1. Some source sends exactly 8 to some block and that block receives exactly 512.
All inputs are finite; a program needn't handle non-finite values.
Results may differ from the reference program's by a relative error of at most 0.04.
Values may be sent and summed in bfloat16 or wider, within the bound.
A program may use at most 128 MiB of HBM per device.

```python
import math
import jax
import jax.numpy as jnp
from jax import lax

D = 768
H = 16
HEAD_WIDTH = 48
DT = 1536
DILATION_STEP = 8
SLIDE_POSITIONS = 512
SLIDES = 8
BLOCKS = 16
GROUP = 128
CAP = 8
LENGTH = 8192
REPORTS = 1024
FEAT_PART = 384
N_REP = 4


def draw_tile_counts(key, part):
    subkeys = jax.random.split(key, 5)
    pair_count = GROUP // 2
    floor_count = jax.random.randint(subkeys[0], (GROUP, 1), 0, CAP + 1)
    spread = jax.random.randint(subkeys[1], (GROUP, pair_count), 0, CAP + 1)
    pair_total = floor_count + spread * (CAP - floor_count + 1) // (CAP + 1)
    leading = jnp.maximum(pair_total[:, :1], 1)
    pair_total = jnp.concatenate([leading, pair_total[:, 1:]], axis=1)
    full_row = jax.random.randint(subkeys[2], (), 0, GROUP)
    row_ids = jnp.arange(GROUP)[:, None]
    pair_total = jnp.where(row_ids == full_row, CAP, pair_total)
    divide = jax.random.randint(subkeys[3], (GROUP, pair_count), 0, CAP + 1)
    first_part = divide * (pair_total + 1) // (CAP + 1)
    peak_col = jax.random.randint(subkeys[4], (), 0, pair_count)
    col_ids = jnp.arange(pair_count)[None, :]
    first_part = jnp.where((row_ids == full_row) & (col_ids == peak_col), CAP, first_part)
    second_part = pair_total - first_part
    counts_all = jnp.stack([first_part, second_part], axis=-1).reshape(GROUP, GROUP)
    return counts_all.reshape(SLIDES, BLOCKS, GROUP).astype(jnp.int32)


def gain_values(key):
    noises = jax.random.normal(jax.random.fold_in(key, 7002), (D,), jnp.float32)
    return jnp.clip(1.0 + 0.18 * noises, 0.1, 1.9)


def draw_tile_feats(key, part):
    own_key = jax.random.fold_in(key, 7101)
    noises = jax.random.normal(own_key, (GROUP, GROUP, CAP, DT), jnp.float32)
    return jnp.clip(noises, -6.0, 6.0).astype(jnp.bfloat16)


def draw_in_weight(key, part):
    own_key = jax.random.fold_in(key, 7102)
    value_rows = jnp.clip(jax.random.normal(own_key, (DT, D), jnp.float32), -6.0, 6.0) * DT ** (-0.5)
    return value_rows.astype(jnp.bfloat16)


def draw_qkv_weight(key, part):
    own_key = jax.random.fold_in(key, 7103)
    qkv_width = H * HEAD_WIDTH
    value_rows = jnp.clip(jax.random.normal(own_key, (D, 3, qkv_width), jnp.float32), -6.0, 6.0) * (1.8 * D ** (-0.5))
    return value_rows.astype(jnp.bfloat16)


def draw_final_gain(key, part):
    return gain_values(key).astype(jnp.float32)


def draw_reports(key, part):
    own_key = jax.random.fold_in(key, 7104)
    value_rows = jnp.clip(jax.random.normal(own_key, (REPORTS, D), jnp.float32), -6.0, 6.0)
    return value_rows.astype(jnp.bfloat16)


def with_ends(values, key, least, high):
    place = [jax.random.randint(jax.random.fold_in(key, axis), (), 0, length) for axis, length in enumerate(values.shape)]
    longest = values.shape.index(max(values.shape))
    beside = place[:longest] + [(place[longest] + 1) % values.shape[longest]] + place[longest + 1:]
    return values.at[tuple(place)].set(least).at[tuple(beside)].set(high)


def block_levels(rng, shape, shards, smallest, high):
    level = 1.0
    for position, parts in shards:
        steps = jax.random.uniform(jax.random.fold_in(jax.random.fold_in(rng, 6), position), (parts,), jnp.float32, smallest / len(shards), high / len(shards))
        level = level * jnp.repeat(jnp.exp(steps), shape[position] // parts).reshape((-1,) + (1,) * (len(shape) - 1 - position))
    return level


def scatter_about(stream_key, shape, deviation, most, cuts=(), kind=jnp.bfloat16):
    loudness = block_levels(stream_key, shape, cuts, -0.22, 0.18) if cuts else 1.0
    entries = jax.random.normal(stream_key, shape, jnp.float32) * deviation * loudness
    return jnp.minimum(jnp.maximum(entries, -most), most).astype(kind)


def setup_inputs(seed: int = 0) -> dict:
    seeds = jax.random.split(jax.random.key(seed), 10)
    return {
        "tile_feats": draw_tile_feats(jax.random.fold_in(seeds[9], 71), 0),
        "tile_counts": draw_tile_counts(jax.random.fold_in(seeds[9], 71), 0),
        "in_weight": draw_in_weight(jax.random.fold_in(seeds[9], 71), 0),
        "norm_gain": jnp.clip(1.0 + 0.18 * jax.random.normal(seeds[3], (D,), jnp.float32), 0.1, 1.9),
        "qkv_weight": draw_qkv_weight(jax.random.fold_in(seeds[9], 71), 0),
        "out_weight": scatter_about(seeds[5], (H * HEAD_WIDTH, D), (H * HEAD_WIDTH) ** -0.5, 0.21875, ((0, 4),)),
        "final_gain": draw_final_gain(jax.random.fold_in(seeds[9], 71), 0),
        "reports": draw_reports(jax.random.fold_in(seeds[9], 71), 0),
        "report_pair": with_ends(jax.random.randint(seeds[8], (SLIDES,), 0, REPORTS), jax.random.fold_in(seeds[8], 1), 0, REPORTS - 1).astype(jnp.int32),
    }


epsilon = 1e-05
logit_scale = 100.0

def layer_norm(value_rows, gain):
    average = lax.optimization_barrier(jnp.mean(value_rows, axis=-1, keepdims=True))
    centred = value_rows - average
    variance = lax.optimization_barrier(jnp.mean(centred * centred, axis=-1, keepdims=True))
    return centred / jnp.sqrt(variance + epsilon) * gain

def compact_rows(buffer, counts_col, capacity, row_total):
    sources = counts_col.shape[0]
    run_ends = jnp.cumsum(counts_col, dtype=jnp.int32)
    starts = run_ends - counts_col
    positions = jnp.arange(row_total, dtype=jnp.int32)
    passed = (run_ends[None, :] <= positions[:, None]).astype(jnp.int32)
    source = jnp.minimum(lax.optimization_barrier(jnp.sum(passed, axis=1, dtype=jnp.int32)), sources - 1)
    chosen_rows = jnp.arange(sources, dtype=jnp.int32)[None, :] == source[:, None]
    offset_in = lax.optimization_barrier(jnp.sum(jnp.where(chosen_rows, starts[None, :], 0), axis=1, dtype=jnp.int32))
    living = positions < run_ends[sources - 1]
    slot_ids = jnp.where(living, source * capacity + positions - offset_in, 0).astype(jnp.int32)
    taken = jnp.take(buffer, slot_ids, axis=0)
    return (jnp.where(living[:, None], taken, jnp.zeros_like(taken)), living)

def pick_rows(value_rows, start_offset):
    reshaped_rows = value_rows.reshape((value_rows.shape[0] // DILATION_STEP, DILATION_STEP) + value_rows.shape[1:])
    return lax.dynamic_index_in_dim(reshaped_rows, start_offset, axis=1, keepdims=False)

def put_rows(value_rows, update, start_offset):
    reshaped_rows = value_rows.reshape((value_rows.shape[0] // DILATION_STEP, DILATION_STEP) + value_rows.shape[1:])
    merged = lax.dynamic_update_index_in_dim(reshaped_rows, jnp.expand_dims(update, 1), start_offset, 1)
    return merged.reshape(value_rows.shape)

def attend_block(queries, key_near, value_near, live_near, key_far, value_far, live_far, start_offset):
    factor = 1.0 / math.sqrt(queries.shape[1])
    near = jnp.dot(queries, key_near.T, preferred_element_type=jnp.float32) * factor
    near = jnp.where(live_near[None, :], near, -jnp.inf)
    picked = pick_rows(queries, start_offset)
    distant = jnp.dot(picked, key_far.T, preferred_element_type=jnp.float32) * factor
    distant = jnp.where(live_far[None, :], distant, -jnp.inf)
    top_near = lax.optimization_barrier(jnp.max(near, axis=1))
    top_far = jnp.maximum(pick_rows(top_near, start_offset), lax.optimization_barrier(jnp.max(distant, axis=1)))
    top_all = put_rows(top_near, top_far, start_offset)
    exp_near = jnp.exp(near - top_all[:, None])
    exp_far = jnp.exp(distant - top_far[:, None])
    sum_near = lax.optimization_barrier(jnp.sum(exp_near, axis=1))
    sum_far = pick_rows(sum_near, start_offset) + lax.optimization_barrier(jnp.sum(exp_far, axis=1))
    sum_all = put_rows(sum_near, sum_far, start_offset)
    weight_near = (exp_near / sum_all[:, None]).astype(jnp.bfloat16)
    weight_far = (exp_far / sum_far[:, None]).astype(jnp.bfloat16)
    result = jnp.dot(weight_near, value_near, preferred_element_type=jnp.float32)
    result_far = pick_rows(result, start_offset) + jnp.dot(weight_far, value_far, preferred_element_type=jnp.float32)
    result = put_rows(result, result_far, start_offset)
    return jnp.where(live_near[:, None], result, jnp.zeros_like(result))

def reference(tile_feats, tile_counts, in_weight, norm_gain, qkv_weight, out_weight, final_gain, reports, report_pair):
    counts_flat = tile_counts.reshape(GROUP, GROUP)

    def receive(target):
        buffer = lax.dynamic_index_in_dim(tile_feats, target, axis=1, keepdims=False).reshape(GROUP * CAP, DT)
        counts_col = lax.dynamic_index_in_dim(counts_flat, target, axis=0, keepdims=False)
        gathered, living = compact_rows(buffer, counts_col, CAP, SLIDE_POSITIONS)
        summed = jnp.zeros((SLIDE_POSITIONS, D), jnp.float32)
        for part_idx in range(N_REP):
            low_col = part_idx * FEAT_PART
            partial_sum = jnp.dot(gathered[:, low_col:low_col + FEAT_PART], in_weight[low_col:low_col + FEAT_PART], preferred_element_type=jnp.float32)
            rounded = lax.optimization_barrier(partial_sum.astype(jnp.bfloat16))
            summed = summed + rounded.astype(jnp.float32)
        return (summed, living)
    feats, living = lax.map(receive, jnp.arange(GROUP, dtype=jnp.int32))
    feats = feats.reshape(SLIDES, LENGTH, D)
    living = living.reshape(SLIDES, LENGTH)
    weight_flat = qkv_weight.reshape(D, 3 * H * HEAD_WIDTH)

    def encode(slide_idx):
        slide_feats = lax.dynamic_index_in_dim(feats, slide_idx, axis=0, keepdims=False)
        slide_live = lax.dynamic_index_in_dim(living, slide_idx, axis=0, keepdims=False)
        normed = layer_norm(slide_feats, norm_gain).astype(jnp.bfloat16)
        projected_rows = jnp.dot(normed, weight_flat, preferred_element_type=jnp.float32).astype(jnp.bfloat16)
        projected_rows = projected_rows.reshape(LENGTH, 3, H, HEAD_WIDTH)

        def one_head(head_index):
            start_offset = (head_index % DILATION_STEP).astype(jnp.int32)
            queries = lax.dynamic_index_in_dim(projected_rows[:, 0], head_index, axis=1, keepdims=False)
            key_all = lax.dynamic_index_in_dim(projected_rows[:, 1], head_index, axis=1, keepdims=False)
            value_all = lax.dynamic_index_in_dim(projected_rows[:, 2], head_index, axis=1, keepdims=False)
            key_far = pick_rows(key_all, start_offset)
            value_far = pick_rows(value_all, start_offset)
            live_far = pick_rows(slide_live, start_offset)

            def one_block(block_idx):
                first_row = block_idx * SLIDE_POSITIONS
                return attend_block(lax.dynamic_slice_in_dim(queries, first_row, SLIDE_POSITIONS, 0), lax.dynamic_slice_in_dim(key_all, first_row, SLIDE_POSITIONS, 0), lax.dynamic_slice_in_dim(value_all, first_row, SLIDE_POSITIONS, 0), lax.dynamic_slice_in_dim(slide_live, first_row, SLIDE_POSITIONS, 0), key_far, value_far, live_far, start_offset)
            return lax.map(one_block, jnp.arange(BLOCKS, dtype=jnp.int32)).reshape(LENGTH, HEAD_WIDTH)
        per_head = lax.map(one_head, jnp.arange(H, dtype=jnp.int32))
        head_rows = jnp.transpose(per_head, (1, 0, 2)).reshape(LENGTH, H * HEAD_WIDTH)
        feat_sum = lax.optimization_barrier(jnp.sum(slide_feats, axis=0))
        head_sum = lax.optimization_barrier(jnp.sum(head_rows, axis=0))
        pooled = (feat_sum + jnp.dot(head_sum, out_weight.astype(jnp.float32), precision=lax.Precision.HIGHEST)) / jnp.sum(slide_live.astype(jnp.float32))
        return (head_rows, layer_norm(pooled, final_gain))
    head_out, slide_emb = lax.map(encode, jnp.arange(SLIDES, dtype=jnp.int32))
    emb_norm = jnp.sqrt(lax.optimization_barrier(jnp.sum(slide_emb * slide_emb, axis=1, keepdims=True)) + 1e-06)
    unit_rows = slide_emb / emb_norm
    report_f = reports.astype(jnp.float32)
    inverse = 1.0 / jnp.sqrt(lax.optimization_barrier(jnp.sum(report_f * report_f, axis=1)) + 1e-06)
    logits = logit_scale * jnp.dot(unit_rows, report_f.T, precision=lax.Precision.HIGHEST) * inverse[None, :]
    highest = lax.optimization_barrier(jnp.max(logits, axis=1))
    log_mass = highest + jnp.log(lax.optimization_barrier(jnp.sum(jnp.exp(logits - highest[:, None]), axis=1)))
    positive = jnp.take_along_axis(logits, report_pair[:, None].astype(jnp.int32), axis=1)[:, 0]
    return (head_out, slide_emb, log_mass - positive)
```

```python
import functools
import math

import jax
import jax.numpy as jnp
from jax import lax
from jax.experimental import pallas as pl
from jax.experimental.pallas import tpu as pltpu
from jax.sharding import PartitionSpec as P

HEAD_WIDTH = 48
STEP = 8
EPS = 1e-05
LOGIT_SCALE = 100.0
NEG = -1e30
MESH = pl.DeviceIdType.MESH
F32 = jnp.float32
BF16 = jnp.bfloat16


def to_peer(src, dst, send, recv, axis, peer):
    return pltpu.make_async_remote_copy(
        src_ref=src, dst_ref=dst, send_sem=send, recv_sem=recv,
        device_id={axis: peer}, device_id_type=MESH,
    )


def share(buf, send, recv, axis, me, n):
    def one(d, _):
        to_peer(buf.at[me], buf.at[me], send.at[d], recv.at[me], axis, lax.rem(me + d, n)).start()
        return 0

    lax.fori_loop(1, n, one, 0)


def shared(buf, send, recv, axis, me, n):
    def one(d, _):
        slot = lax.rem(me + d, n)
        to_peer(buf.at[me], buf.at[slot], send.at[d], recv.at[slot], axis, slot).wait()
        return 0

    lax.fori_loop(1, n, one, 0)


def encoder_kernel(
    n_seq, n_rep,
    feats_ref, counts_ref, gain_ref, wqkv_ref, wout_ref, fgain_ref, reports_ref, pair_ref,
    out_ref, emb_ref, loss_ref,
    normed, q_s, k_s, v_s, kv_all, m_s, l_s, outn, natural, fbuf, hbuf, rbuf, sbuf,
    kv_recv, right_send, left_send, f_send, f_recv, h_send, h_recv, r_send, r_recv, s_send, s_recv,
):
    seq = lax.axis_index("seq")
    rep = lax.axis_index("rep")
    rows, width = normed.shape
    heads = m_s.shape[0]
    part = heads * HEAD_WIDTH
    lattice = rows // STEP
    wide = q_s.shape[1]
    scale = math.log2(math.e) / math.sqrt(HEAD_WIDTH)
    chunk = 128
    half = lax.rem(rep * heads, STEP) * lattice
    far_rows = heads * lattice

    barrier = pltpu.get_barrier_semaphore()

    def greet(axis, me, n):
        def one(d, _):
            pl.semaphore_signal(barrier, inc=1, device_id={axis: lax.rem(me + d, n)}, device_id_type=MESH)
            return 0

        lax.fori_loop(1, n, one, 0)

    greet("seq", seq, n_seq)
    greet("rep", rep, n_rep)

    counts = counts_ref[...].astype(F32)
    blocks = lax.broadcasted_iota(jnp.int32, counts.shape, 0)
    own_total = jnp.sum(jnp.where(blocks == seq, counts, 0.0), keepdims=True)
    slide_total = jnp.sum(counts, keepdims=True)

    def norm_rows(start):
        values = feats_ref[pl.ds(start, chunk), :].astype(F32)
        centred = values - jnp.mean(values, axis=1, keepdims=True)
        variance = jnp.mean(centred * centred, axis=1, keepdims=True)
        normed[pl.ds(start, chunk), :] = (centred * lax.rsqrt(variance + EPS) * gain_ref[...]).astype(BF16)
        return jnp.sum(values, axis=0, keepdims=True)

    feat_sum = jnp.zeros((1, width), F32)
    for index in range(far_rows // chunk):
        feat_sum += norm_rows(pl.multiple_of(half + index * chunk, chunk))

    far_kv = jnp.dot(
        normed[pl.ds(pl.multiple_of(half, far_rows), far_rows), :], wqkv_ref[:, wide:],
        preferred_element_type=F32,
    )
    lane = lax.broadcasted_iota(jnp.int32, (1, wide), 1)
    far_k = jnp.zeros((lattice, wide), F32)
    far_v = jnp.zeros((lattice, wide), F32)
    for head in range(heads):
        own = (lane >= head * HEAD_WIDTH) & (lane < (head + 1) * HEAD_WIDTH)
        block = far_kv[head * lattice:(head + 1) * lattice]
        far_k = jnp.where(own, block[:, :wide], far_k)
        far_v = jnp.where(own, block[:, wide:], far_v)
    low = lax.broadcasted_iota(jnp.int32, (1, 128), 1) < 64
    mixed = jnp.where(low, far_k[:, 128:], pltpu.roll(far_v[:, 128:], 64, 1))
    kv_all[seq] = jnp.concatenate([far_k[:, :128], mixed, far_v[:, :128]], axis=1).astype(BF16)

    pl.semaphore_wait(barrier, n_seq + n_rep - 2)
    right, left = lax.rem(seq + 1, n_seq), lax.rem(seq + n_seq - 1, n_seq)
    rights, lefts = n_seq // 2, n_seq - 1 - n_seq // 2

    def go_right(step):
        slot = lax.rem(seq - step + n_seq, n_seq)
        return to_peer(kv_all.at[slot], kv_all.at[slot], right_send.at[step], kv_recv.at[slot], "seq", right)

    def go_left(step):
        slot = lax.rem(seq + step, n_seq)
        return to_peer(kv_all.at[slot], kv_all.at[slot], left_send.at[step], kv_recv.at[slot], "seq", left)

    def arrived(slot):
        to_peer(kv_all.at[slot], kv_all.at[slot], right_send.at[0], kv_recv.at[slot], "seq", right).wait_recv()

    go_right(0).start()
    go_left(0).start()

    other = lax.rem(half + far_rows, rows)
    for index in range((rows - far_rows) // chunk):
        feat_sum += norm_rows(pl.multiple_of(other + index * chunk, chunk))
    fbuf[seq] = feat_sum
    share(fbuf, f_send, f_recv, "seq", seq, n_seq)

    row_id = lax.broadcasted_iota(jnp.int32, (rows, 1), 0)
    position = lax.rem(row_id, lattice) * STEP + lax.div(row_id, lattice)
    live_rows = position.astype(F32) < own_total

    def project(index, _):
        at = pl.ds(pl.multiple_of(index * chunk, chunk), chunk)
        three = jnp.dot(normed[at, :], wqkv_ref[...], preferred_element_type=F32)
        ids = lax.broadcasted_iota(jnp.int32, (chunk, 1), 0) + index * chunk
        place = lax.rem(ids, lattice) * STEP + lax.div(ids, lattice)
        bias = jnp.where(place.astype(F32) < own_total, 0.0, NEG)
        q_s[at, :] = jnp.where(lane == part, 1.0, three[:, :wide]).astype(BF16)
        k_s[at, :] = jnp.where(lane == part, bias, three[:, wide:2 * wide]).astype(BF16)
        v_s[at, :] = jnp.where(lane == part, 1.0, three[:, 2 * wide:]).astype(BF16)
        return 0

    lax.fori_loop(0, rows // chunk, project, 0)
    outn[...] = jnp.zeros_like(outn)

    def near(piece):
        head = lax.div(piece, rows // chunk)
        at = pl.ds(pl.multiple_of(lax.rem(piece, rows // chunk) * chunk, chunk), chunk)
        own = (lane >= head * HEAD_WIDTH) & (lane < (head + 1) * HEAD_WIDTH)
        queries = q_s[at, :]
        queries = jnp.where(own | (lane == part), queries, jnp.zeros_like(queries))
        scores = lax.dot_general(queries, k_s[...], (((1,), (1,)), ((), ())), preferred_element_type=F32)
        top = jnp.max(scores, axis=1, keepdims=True)
        weights = jnp.exp2((scores - top) * scale).astype(BF16)
        result = jnp.dot(weights, v_s[...], preferred_element_type=F32)
        mass = jnp.sum(jnp.where(lane == part, result, 0.0), axis=1, keepdims=True)
        m_s[head, at, :] = top
        l_s[head, at, :] = mass
        outn[at, :] = jnp.where(own, result * (1.0 / mass), outn[at, :])

    pieces = heads * (rows // chunk)
    per_step = pieces // rights

    def ring(step, _):
        @pl.when(step >= 1)
        def _():
            arrived(lax.rem(seq - step + n_seq, n_seq))
            go_right(step).start()

            @pl.when(step <= lefts)
            def _():
                arrived(lax.rem(seq + step, n_seq))

            @pl.when(step < lefts)
            def _():
                go_left(step).start()

        for index in range(per_step):
            near(step * per_step + index)
        return 0

    lax.fori_loop(0, rights, ring, 0)

    keys = n_seq * lattice
    key_block = lax.broadcasted_iota(jnp.int32, (n_seq, keys), 1) // lattice
    block_id = lax.broadcasted_iota(jnp.int32, (n_seq, keys), 0)
    spread = jnp.where(key_block == block_id, 1.0, 0.0).astype(BF16)
    wide_counts = lax.dot_general(counts.astype(BF16), spread, (((0,), (0,)), ((), ())), preferred_element_type=F32)
    key_total = jnp.dot(jnp.ones((8, counts.shape[1]), BF16), wide_counts.astype(BF16), preferred_element_type=F32)[:1]
    key_place = (lax.rem(lax.broadcasted_iota(jnp.int32, (1, keys), 1), lattice) * STEP).astype(F32)
    report_rows = reports_ref[...].astype(F32)
    inverse = LOGIT_SCALE * lax.rsqrt(jnp.sum(report_rows * report_rows, axis=1, keepdims=True) + 1e-06)

    arrived(lax.rem(seq - rights + n_seq, n_seq))

    keys_far = kv_all[...].reshape(keys, 3 * 128)
    for head in range(heads):
        own = (lane >= head * HEAD_WIDTH) & (lane < (head + 1) * HEAD_WIDTH)
        start = pl.multiple_of(half + head * lattice, lattice)
        at = pl.ds(start, lattice)
        queries = q_s[at, :]
        queries = jnp.where(own, queries, jnp.zeros_like(queries))
        scores = lax.dot_general(queries, keys_far[:, :wide], (((1,), (1,)), ((), ())), preferred_element_type=F32)
        offset = lax.div(start, lattice).astype(F32)
        scores = jnp.where(key_place + offset < key_total, scores, NEG)
        top_far = jnp.max(scores, axis=1, keepdims=True)
        weights = jnp.exp2((scores - top_far) * scale)
        mass_far = jnp.sum(weights, axis=1, keepdims=True)
        mixed = jnp.dot(weights.astype(BF16), keys_far[:, 128:], preferred_element_type=F32)
        result = jnp.concatenate([mixed[:, 128:], pltpu.roll(mixed[:, :128], 64, 1)], axis=1)
        top_near = m_s[head, at, :]
        top = jnp.maximum(top_near, top_far)
        keep_near = l_s[head, at, :] * jnp.exp2((top_near - top) * scale)
        keep_far = jnp.exp2((top_far - top) * scale)
        inverse_mass = 1.0 / (keep_near + mass_far * keep_far)
        before = outn[at, :]
        merged = before * (keep_near * inverse_mass) + result * (keep_far * inverse_mass)
        outn[at, :] = jnp.where(own, merged, before)

    final = jnp.where(live_rows, outn[...], 0.0)
    hbuf[seq] = jnp.sum(final, axis=0, keepdims=True)
    share(hbuf, h_send, h_recv, "seq", seq, n_seq)
    for offset in range(STEP):
        for tile in range(wide // 128):
            natural[tile, pl.ds(offset, lattice, stride=STEP), :] = final[
                offset * lattice:(offset + 1) * lattice, tile * 128:(tile + 1) * 128
            ]
    for tile in range(wide // 128):
        end = min(part, (tile + 1) * 128)
        out_ref[:, tile * 128:end] = natural[tile, :, :end - tile * 128]
    shared(fbuf, f_send, f_recv, "seq", seq, n_seq)
    feat_total = jnp.sum(fbuf[...], axis=0)
    shared(hbuf, h_send, h_recv, "seq", seq, n_seq)
    head_total = jnp.sum(hbuf[...], axis=0)
    high = head_total.astype(BF16)
    rest = head_total - high.astype(F32)
    middle = rest.astype(BF16)
    lowest = (rest - middle.astype(F32)).astype(BF16)
    row8 = lax.broadcasted_iota(jnp.int32, (8, wide), 0)
    stacked = jnp.where(row8 == 0, high.astype(F32), 0.0)
    stacked = jnp.where(row8 == 1, middle.astype(F32), stacked)
    stacked = jnp.where(row8 == 2, lowest.astype(F32), stacked).astype(BF16)
    term = jnp.sum(jnp.dot(stacked[:, :part], wout_ref[...], preferred_element_type=F32), axis=0, keepdims=True)
    rbuf[rep] = term
    share(rbuf, r_send, r_recv, "rep", rep, n_rep)
    shared(rbuf, r_send, r_recv, "rep", rep, n_rep)
    pooled = (feat_total + jnp.sum(rbuf[...], axis=0)) / slide_total
    centred = pooled - jnp.mean(pooled, axis=1, keepdims=True)
    variance = jnp.mean(centred * centred, axis=1, keepdims=True)
    emb = centred / jnp.sqrt(variance + EPS) * fgain_ref[...]
    emb_ref[...] = emb
    unit = emb / jnp.sqrt(jnp.sum(emb * emb, axis=1, keepdims=True) + 1e-06)
    logits = jnp.sum(report_rows * unit, axis=1, keepdims=True) * inverse
    ids = lax.broadcasted_iota(jnp.int32, logits.shape, 0) + rep * logits.shape[0]
    positive = jnp.sum(jnp.where(ids == pair_ref[0], logits, 0.0), keepdims=True)
    top = jnp.max(logits, keepdims=True)
    mass = jnp.sum(jnp.exp(logits - top), keepdims=True)
    lane1 = lax.broadcasted_iota(jnp.int32, (1, 128), 1)
    sbuf[rep] = jnp.where(lane1 == 0, top, jnp.where(lane1 == 1, mass, jnp.where(lane1 == 2, positive, 0.0)))
    share(sbuf, s_send, s_recv, "rep", rep, n_rep)
    shared(sbuf, s_send, s_recv, "rep", rep, n_rep)
    every = sbuf[...]
    tops, masses, positives = every[:, :, 0:1], every[:, :, 1:2], every[:, :, 2:3]
    highest = jnp.max(tops, axis=0)
    total = jnp.sum(masses * jnp.exp(tops - highest[None]), axis=0)
    loss_ref[...] = highest + jnp.log(total) - jnp.sum(positives, axis=0)

    def sent_right(step, _):
        go_right(step).wait_send()
        return 0

    def sent_left(step, _):
        go_left(step).wait_send()
        return 0

    lax.fori_loop(0, rights, sent_right, 0)
    lax.fori_loop(0, lefts, sent_left, 0)


def encoder(n_seq, n_rep, feats, counts, gain, wqkv, wout, fgain, reports, pair):
    rows, width = feats.shape
    part = wout.shape[0]
    heads = part // HEAD_WIDTH
    wide = wqkv.shape[1] // 3
    lattice = rows // STEP
    dma = pltpu.SemaphoreType.DMA
    vmem = pl.BlockSpec(memory_space=pltpu.VMEM)
    return pl.pallas_call(
        functools.partial(encoder_kernel, n_seq, n_rep),
        out_shape=(
            jax.ShapeDtypeStruct((rows, part), F32),
            jax.ShapeDtypeStruct((1, width), F32),
            jax.ShapeDtypeStruct((1, 1), F32),
        ),
        in_specs=[vmem] * 7 + [pl.BlockSpec(memory_space=pltpu.SMEM)],
        out_specs=(vmem, vmem, vmem),
        scratch_shapes=[
            pltpu.VMEM((rows, width), BF16),
            pltpu.VMEM((rows, wide), BF16),
            pltpu.VMEM((rows, wide), BF16),
            pltpu.VMEM((rows, wide), BF16),
            pltpu.VMEM((n_seq, lattice, 3 * 128), BF16),
            pltpu.VMEM((heads, rows, 1), F32),
            pltpu.VMEM((heads, rows, 1), F32),
            pltpu.VMEM((rows, wide), F32),
            pltpu.VMEM((wide // 128, rows, 128), F32),
            pltpu.VMEM((n_seq, 1, width), F32),
            pltpu.VMEM((n_seq, 1, wide), F32),
            pltpu.VMEM((n_rep, 1, width), F32),
            pltpu.VMEM((n_rep, 1, 128), F32),
            dma((n_seq,)),
            dma((n_seq,)),
            dma((n_seq,)),
            dma((n_seq,)),
            dma((n_seq,)),
            dma((n_seq,)),
            dma((n_seq,)),
            dma((n_rep,)),
            dma((n_rep,)),
            dma((n_rep,)),
            dma((n_rep,)),
        ],
        compiler_params=pltpu.CompilerParams(
            collective_id=0, has_side_effects=True, vmem_limit_bytes=48 * 1024 * 1024
        ),
    )(feats, counts, gain, wqkv, wout, fgain, reports, pair)


def compact_rows(buffer, counts_col, capacity, row_total):
    sources = counts_col.shape[0]
    run_ends = jnp.cumsum(counts_col, dtype=jnp.int32)
    starts = run_ends - counts_col
    order = jnp.arange(row_total, dtype=jnp.int32)
    lattice = row_total // STEP
    positions = (order % lattice) * STEP + order // lattice
    passed = (run_ends[None, :] <= positions[:, None]).astype(jnp.int32)
    source = jnp.minimum(jnp.sum(passed, axis=1, dtype=jnp.int32), sources - 1)
    chosen_rows = jnp.arange(sources, dtype=jnp.int32)[None, :] == source[:, None]
    offset_in = jnp.sum(jnp.where(chosen_rows, starts[None, :], 0), axis=1, dtype=jnp.int32)
    living = positions < run_ends[sources - 1]
    slot_ids = jnp.where(living, source * capacity + positions - offset_in, 0)
    taken = jnp.take(buffer, slot_ids, axis=0)
    return jnp.where(living[:, None], taken, jnp.zeros_like(taken))


def local(tile_feats, tile_counts, in_weight, norm_gain, qkv_weight, out_weight, final_gain, reports, report_pair):
    sources, capacity, feat_group = tile_feats.shape[1:]
    rows = 512
    width = out_weight.shape[1]
    part = qkv_weight.shape[2]
    wide = -(-part // 128) * 128
    counts = tile_counts.reshape(tile_counts.shape[1], sources)
    own_counts = lax.dynamic_index_in_dim(counts, lax.axis_index("seq"), axis=0, keepdims=False)
    arrived = lax.all_to_all(tile_feats, ("slide", "seq"), split_axis=1, concat_axis=0, tiled=True)
    gathered = compact_rows(arrived.reshape(sources * capacity, feat_group), own_counts, capacity, rows)
    partial_sum = jnp.dot(gathered, in_weight, preferred_element_type=F32)
    feats = lax.psum(partial_sum.astype(BF16), "rep")
    wqkv = jnp.pad(qkv_weight, ((0, 0), (0, 0), (0, wide - part))).reshape(width, 3 * wide)
    head_out, emb, loss = encoder(
        lax.axis_size("seq"), lax.axis_size("rep"), feats, counts, norm_gain.reshape(1, width), wqkv,
        out_weight, final_gain.reshape(1, width), reports, report_pair,
    )
    return head_out[None], emb, loss.reshape(1)


def solution(mesh):
    in_specs = (
        P(("slide", "seq"), None, None, "rep"),
        P("slide", None, None),
        P("rep", None),
        P(),
        P(None, None, "rep"),
        P("rep", None),
        P(),
        P("rep", None),
        P("slide"),
    )
    out_specs = (P("slide", "seq", "rep"), P("slide", None), P("slide"))
    return jax.shard_map(local, mesh=mesh, in_specs=in_specs, out_specs=out_specs, check_vma=False)
```
